32 devices in a mesh: vp: 16 (over z, y, x), op: 2 (over core).
Axes of the slice: x: 2, y: 2, z: 4, core: 2. Of those that a mesh axis runs over, the one named last changes fastest.
Arguments:
- multipliers: bfloat16 [2048, 131072], P('op', 'vp'), may hold values from -6 to 6
- integrals: bfloat16 [131072, 1024], P('vp'), may hold values from -0.0234375 to 0.0234375
- amplitudes: bfloat16 [2048, 131072], P('op', 'vp'), may hold values from -0.09375 to 0.09375
- slab_multipliers: bfloat16 [1024, 2048], P('vp', 'op'), may hold values from -6 to 6
- slab_amplitudes: bfloat16 [1024, 2048], P('vp', 'op'), may hold values from -0.09375 to 0.09375
- residual_rest: bfloat16 [1024, 2048], P('vp', 'op'), may hold values from -6 to 6
- occupied_energy: bfloat16 [2048], P('op'), may hold values from -2.5 to -0.5
- virtual_energy: bfloat16 [1024], P('vp'), may hold values from 1 to 4
Outputs:
- updated_multipliers: bfloat16 [1024, 2048], P('vp', 'op')
- pair_density: bfloat16 [1024, 131072], P('op', 'vp')
The draws below stay inside these ranges and needn't reach their ends.
All inputs are finite; a program needn't handle non-finite values.
Results may differ from the reference program's by a relative error of at most 0.004.
Values may be sent and summed in bfloat16 or wider, within the bound.
No kernel may reach another device: no remote copies, remote signals or barrier semaphores. Data moves between devices by JAX's collectives and lax.ppermute only.
A program may use at most 192 MiB of HBM per device.

```python
import jax
import jax.numpy as jnp
from jax import lax

P_SIZE = 2048
Q = 131072
SLAB_PAIRS = 1024


def with_spikes(entries, stream_key, source, target, parts, factor):
    owner, partner = [(jnp.arange(entries.shape[dim]) // (entries.shape[dim] // parts)).reshape([-1 if axis == dim else 1 for axis in range(entries.ndim)]) for dim in (source, target)]
    chosen = jax.random.permutation(stream_key, parts)[partner]
    strong = (owner == chosen) | (owner == (partner + parts // 2) % parts)
    return jnp.where(strong, factor * entries, entries)


def block_levels(key, extent, pieces, smallest, top_value):
    def one(position, parts):
        draws = jax.random.uniform(jax.random.fold_in(jax.random.fold_in(key, 6), position), (parts,), jnp.float32, smallest / len(pieces), top_value / len(pieces))
        return jnp.repeat(jnp.exp(draws), extent[position] // parts).reshape((-1,) + (1,) * (len(extent) - position - 1))

    level = one(*pieces[0])
    for cut in pieces[1:]:
        level = level * one(*cut)
    return level


def centred(stream_key, dims, deviation, reach, cuts=(), held_as=jnp.bfloat16):
    gain = block_levels(stream_key, dims, cuts, -0.22, 0.18) if cuts else 1.0
    result = jax.random.normal(stream_key, dims, jnp.float32) * deviation * gain
    return jnp.minimum(jnp.maximum(result, -reach), reach).astype(held_as)


def heavy_noise(rng, shape, deviation, most, shards, heavy, held_as=jnp.bfloat16):
    drawn = deviation * jax.random.normal(rng, shape, jnp.float32)
    if shards:
        drawn = drawn * block_levels(rng, shape, shards, -0.22, 0.18)
    return jnp.clip(with_spikes(drawn, jax.random.fold_in(rng, 3), *heavy), -most, most).astype(held_as)


def setup_inputs(seed: int = 0) -> dict:
    seeds = jax.random.split(jax.random.key(seed), 9)
    multipliers = centred(seeds[0], (P_SIZE, Q), 1.0, 6.0, ((0, 2), (1, 16)))
    integrals = heavy_noise(seeds[1], (Q, SLAB_PAIRS), Q ** -0.5, 0.0234375, ((0, 16),), (0, 1, 16, 2.0))
    amplitudes = centred(seeds[2], (P_SIZE, Q), (1.0 / (2 * P_SIZE) ** 0.5), 0.09375, ((0, 2), (1, 16)))
    slab_multipliers = centred(seeds[3], (SLAB_PAIRS, P_SIZE), 1.0, 6.0, ((0, 16), (1, 2)))
    slab_amplitudes = centred(seeds[4], (SLAB_PAIRS, P_SIZE), (1.0 / (2 * P_SIZE) ** 0.5), 0.09375, ((0, 16), (1, 2)))
    residual_rest = centred(seeds[5], (SLAB_PAIRS, P_SIZE), 1.0, 6.0, ((0, 16), (1, 2)))
    occupied_energy = jnp.clip(-2.5 + 2.0 * jax.random.uniform(seeds[6], (P_SIZE,), jnp.float32) ** block_levels(seeds[6], (P_SIZE,), ((0, 2),), -0.2, 0.2), -2.5, -0.5).astype(jnp.bfloat16)
    virtual_energy = jnp.clip(1.0 + 3.0 * jax.random.uniform(seeds[7], (SLAB_PAIRS,), jnp.float32) ** block_levels(seeds[7], (SLAB_PAIRS,), ((0, 16),), -0.2, 0.2), 1.0, 4.0).astype(jnp.bfloat16)
    return dict(multipliers=multipliers, integrals=integrals, amplitudes=amplitudes, slab_multipliers=slab_multipliers, slab_amplitudes=slab_amplitudes, residual_rest=residual_rest, occupied_energy=occupied_energy, virtual_energy=virtual_energy)


def reference(multipliers, integrals, amplitudes, slab_multipliers, slab_amplitudes, residual_rest, occupied_energy, virtual_energy):
    ladder = lax.dot_general(integrals, multipliers, (((0,), (1,)), ((), ())), preferred_element_type=jnp.float32)
    divisor = virtual_energy.astype(jnp.float32)[:, None] - occupied_energy.astype(jnp.float32)[None, :]
    renewed = slab_multipliers.astype(jnp.float32) + (ladder + residual_rest.astype(jnp.float32)) / divisor
    renewed = renewed.astype(jnp.bfloat16)
    density = jnp.dot(renewed, amplitudes, preferred_element_type=jnp.float32)
    density = density + jnp.dot(slab_amplitudes, multipliers, preferred_element_type=jnp.float32)
    return renewed, density.astype(jnp.bfloat16)
```

```python
import functools

import jax
import jax.numpy as jnp
from jax import lax
from jax.experimental import pallas as pl
from jax.experimental.pallas import tpu as pltpu
from jax.sharding import PartitionSpec as P

BF16, F32 = jnp.bfloat16, jnp.float32
LANES = 128


def divisor_at_most(extent, wanted):
    while extent % wanted:
        wanted //= 2
    return wanted


class Plan:
    def __init__(self, mesh, slab):
        self.n, self.cores = mesh.shape["vp"], mesh.shape["op"]
        self.bits = self.n.bit_length() - 1
        self.rows = slab // self.n
        top = self.bits - 1
        self.unit = LANES // self.rows
        low = self.unit.bit_length() - 1
        first, second = low, min(low + 1, top - 1)
        between = [b for b in range(self.bits) if b != top]
        up = [b for b in between if b != first]
        down = [b for b in reversed(between) if b != second]
        self.orders = ([first] + up + [top], [second] + down + [top])
        self.top = top

    def exchange(self, x, step):
        pairs = []
        for v in range(self.n):
            for c in range(self.cores):
                peer = v ^ (1 << self.orders[c % 2][step])
                pairs.append((v * self.cores + c, peer * self.cores + c))
        return lax.ppermute(x, ("vp", "op"), pairs)

    def swap(self, x):
        return lax.ppermute(x, "op", [(c, c ^ 1) for c in range(self.cores)])

    def to_other_half(self, x):
        half = self.n // 2
        pairs = []
        for v in range(self.n):
            c = v // half
            pairs.append((v * self.cores + c, (v ^ half) * self.cores + c))
        return lax.ppermute(x, ("vp", "op"), pairs)

    def bit_at(self, core, step):
        return jnp.where(core == 0, self.orders[0][step], self.orders[1][step])


def ladder_half(plan, place, multipliers, integrals, keep):
    pairs, depth = multipliers.shape
    slab = integrals.shape[1]
    blocks = slab // LANES // 2
    tile = divisor_at_most(depth, 2048)
    low = plan.unit.bit_length() - 1

    def which(i, place_ref):
        shift = plan.bit_at(place_ref[1], 0) - low
        own = (place_ref[0] >> (shift + low)) & 1
        bit = own if keep else 1 - own
        rest = i & ((1 << shift) - 1)
        return ((i >> shift) << (shift + 1)) | (bit << shift) | rest

    def kernel(place_ref, m_ref, *refs):
        i_refs, out_ref, total = refs[:blocks], refs[blocks], refs[blocks + 1]
        step = pl.program_id(0)
        part = jnp.dot(
            m_ref[...],
            jnp.concatenate([r[...] for r in i_refs], axis=1),
            preferred_element_type=F32,
        )

        @pl.when(step == 0)
        def _():
            total[...] = part

        @pl.when(step > 0)
        def _():
            total[...] += part

        @pl.when(step == pl.num_programs(0) - 1)
        def _():
            me, core = place_ref[0], place_ref[1]
            for i in range(blocks):
                block = total[:, i * LANES : (i + 1) * LANES].T
                for t in range(plan.unit):
                    away = (which(i, place_ref) * plan.unit + t) ^ me
                    slot = 0
                    for s in range(1, plan.bits):
                        stays = 1 - ((away >> plan.bit_at(core, s)) & 1)
                        slot = slot * 2 + stays
                    out_ref[slot] = block[t * plan.rows : (t + 1) * plan.rows].astype(out_ref.dtype)

    return pl.pallas_call(
        kernel,
        grid_spec=pltpu.PrefetchScalarGridSpec(
            num_scalar_prefetch=1,
            grid=(depth // tile,),
            in_specs=[pl.BlockSpec((pairs, tile), lambda k, p: (0, k))]
            + [
                pl.BlockSpec((tile, LANES), functools.partial(lambda k, p, i: (k, which(i, p)), i=i))
                for i in range(blocks)
            ],
            out_specs=pl.BlockSpec((plan.n // 2, plan.rows, pairs), lambda k, p: (0, 0, 0)),
            scratch_shapes=[pltpu.VMEM((pairs, slab // 2), F32)],
        ),
        out_shape=jax.ShapeDtypeStruct((plan.n // 2, plan.rows, pairs), F32 if keep else BF16),
        compiler_params=pltpu.CompilerParams(vmem_limit_bytes=40 * 2**20),
        cost_estimate=pl.CostEstimate(
            flops=pairs * depth * slab,
            bytes_accessed=2 * (pairs * depth + depth * slab // 2 + pairs * slab),
            transcendentals=0,
        ),
        name="ladder_keep" if keep else "ladder_send",
    )(place, multipliers, *[integrals] * blocks)


def amplitude_part(rows, own, other, piece, pieces, total):
    height, depth = rows.shape
    width = own.shape[1]
    tile = divisor_at_most(width // pieces, 1024)
    steps = width // pieces // tile
    half = depth // 2

    def kernel(l_ref, a_ref, b_ref, *refs):
        refs[-1][...] = jnp.dot(l_ref[:, :half], a_ref[...], preferred_element_type=F32) + jnp.dot(
            l_ref[:, half:], b_ref[...], preferred_element_type=F32
        )

    at = lambda j: (0, piece * steps + j)
    given = [] if total is None else [total]
    return pl.pallas_call(
        kernel,
        grid=(steps,),
        in_specs=[
            pl.BlockSpec((height, depth), lambda j: (0, 0)),
            pl.BlockSpec((half, tile), at),
            pl.BlockSpec((half, tile), at),
        ]
        + [pl.BlockSpec(memory_space=pl.ANY)] * len(given),
        out_specs=pl.BlockSpec((height, tile), at),
        out_shape=jax.ShapeDtypeStruct((height, width), F32),
        input_output_aliases={3: 0} if given else {},
        compiler_params=pltpu.CompilerParams(vmem_limit_bytes=40 * 2**20),
        cost_estimate=pl.CostEstimate(
            flops=2 * height * depth * width // pieces,
            bytes_accessed=2 * depth * width // pieces + 4 * height * width // pieces,
            transcendentals=0,
        ),
        name=f"amplitude_part_{piece}",
    )(rows, own, other, *given)


def density(plan, place, rows, own, other, total):
    height, depth = rows.shape
    width = own.shape[1]
    tile = divisor_at_most(width, 1024)
    half = depth // 2
    blocks = height // plan.rows

    def kernel(place_ref, l_ref, a_ref, b_ref, t_ref, o_ref):
        out = (
            t_ref[...]
            + jnp.dot(l_ref[:, :half], a_ref[...], preferred_element_type=F32)
            + jnp.dot(l_ref[:, half:], b_ref[...], preferred_element_type=F32)
        )
        me, core = place_ref[0], place_ref[1]
        for i in range(blocks):
            slot = me & (blocks - 1)
            for s in range(plan.bits - 1):
                away = (i >> (plan.bits - 2 - s)) & 1
                slot = slot ^ (away << plan.bit_at(core, s))
            o_ref[slot] = out[i * plan.rows : (i + 1) * plan.rows].astype(BF16)

    return pl.pallas_call(
        kernel,
        grid_spec=pltpu.PrefetchScalarGridSpec(
            num_scalar_prefetch=1,
            grid=(width // tile,),
            in_specs=[
                pl.BlockSpec((height, depth), lambda j, p: (0, 0)),
                pl.BlockSpec((half, tile), lambda j, p: (0, j)),
                pl.BlockSpec((half, tile), lambda j, p: (0, j)),
                pl.BlockSpec((height, tile), lambda j, p: (0, j)),
            ],
            out_specs=pl.BlockSpec((blocks, plan.rows, tile), lambda j, p: (0, 0, j)),
        ),
        out_shape=jax.ShapeDtypeStruct((blocks, plan.rows, width), BF16),
        compiler_params=pltpu.CompilerParams(vmem_limit_bytes=40 * 2**20),
        cost_estimate=pl.CostEstimate(
            flops=2 * height * depth * width,
            bytes_accessed=2 * depth * width + 6 * height * width,
            transcendentals=0,
        ),
        name="density",
    )(place, rows, own, other, total).reshape(height, width)


def renew_slab(current, ladder, rest, virtual, occupied):
    divisor = virtual.astype(F32)[:, None] - occupied.astype(F32)[None, :]
    renewed = current.astype(F32) + (ladder + rest.astype(F32)) / divisor
    return renewed.astype(BF16)


def reduce_ladder(plan, kept, sent):
    for step in range(plan.bits):
        arrived = plan.exchange(sent, step)
        total = kept + arrived.astype(F32)
        if step == plan.bits - 1:
            return total.reshape(total.shape[-2:])
        half = total.shape[0] // 2
        sent, kept = total[:half].astype(BF16), total[half:]


def gather_rows(plan, mine):
    core = lax.axis_index("op")
    home = lax.axis_index("vp") // (plan.n // 2)
    both = jnp.concatenate([mine, plan.swap(mine)], axis=1)
    crossed = plan.to_other_half(both)
    rows = jnp.where(core == home, both, crossed)
    for step in range(plan.bits - 2, -1, -1):
        rows = jnp.concatenate([rows, plan.exchange(rows, step)], axis=0)
    return rows


def local(
    plan,
    multipliers,
    integrals,
    amplitudes,
    slab_multipliers,
    slab_amplitudes,
    residual_rest,
    occupied_energy,
    virtual_energy,
):
    place = jnp.stack([lax.axis_index("vp"), lax.axis_index("op")]).astype(jnp.int32)
    their_multipliers = plan.swap(multipliers)
    every_amp = gather_rows(plan, slab_amplitudes)
    sent = ladder_half(plan, place, multipliers, integrals, keep=False)
    kept = ladder_half(plan, place, multipliers, integrals, keep=True)
    their_amplitudes = plan.swap(amplitudes)
    ladder = reduce_ladder(plan, kept, sent)
    renewed = renew_slab(slab_multipliers, ladder, residual_rest, virtual_energy, occupied_energy)
    every_new = gather_rows(plan, renewed)
    total = None
    pieces = 4
    for piece in range(pieces):
        total = amplitude_part(every_amp, multipliers, their_multipliers, piece, pieces, total)
    return renewed, density(plan, place, every_new, amplitudes, their_amplitudes, total)


def solution(mesh):
    def whole(*args):
        plan = Plan(mesh, args[1].shape[1])
        return jax.shard_map(
            functools.partial(local, plan),
            mesh=mesh,
            in_specs=(
                P("op", "vp"),
                P("vp", None),
                P("op", "vp"),
                P("vp", "op"),
                P("vp", "op"),
                P("vp", "op"),
                P("op"),
                P("vp"),
            ),
            out_specs=(P("vp", "op"), P("op", "vp")),
            check_vma=False,
        )(*args)

    return whole
```

```python
import functools

import jax
import jax.numpy as jnp
from jax import lax
from jax.experimental import pallas as pl
from jax.experimental.pallas import tpu as pltpu
from jax.sharding import PartitionSpec as P


BF16, F32 = jnp.bfloat16, jnp.float32
LANES = 128
KERNEL_VMEM = 21 * 2**20


def divisor_at_most(extent, wanted):
    while extent % wanted:
        wanted //= 2
    return wanted


class Plan:
    def __init__(self, mesh, slab):
        self.n, self.cores = mesh.shape["vp"], mesh.shape["op"]
        self.bits = self.n.bit_length() - 1
        self.rows = slab // self.n
        top = self.bits - 1
        self.unit = LANES // self.rows
        low = self.unit.bit_length() - 1
        first, second = low, min(low + 1, top - 1)
        between = [b for b in range(self.bits) if b != top]
        up = [b for b in between if b != first]
        down = [b for b in reversed(between) if b != second]
        self.orders = ([first] + up + [top], [second] + down + [top])
        others = [b for b in between if b not in (first, second)]
        self.early = (
            others[:1] + [second, first] + others[1:] + [top],
            [first, second] + others + [top],
        )

    def exchange(self, x, step, orders=None):
        pairs = []
        for v in range(self.n):
            for c in range(self.cores):
                peer = v ^ (1 << (orders or self.orders)[c % 2][step])
                pairs.append((v * self.cores + c, peer * self.cores + c))
        return lax.ppermute(x, ("vp", "op"), pairs)

    def swap(self, x):
        return lax.ppermute(x, "op", [(c, c ^ 1) for c in range(self.cores)])

    def bit_at(self, core, step, orders=None):
        first, second = (orders or self.orders)[:2]
        return jnp.where(core == 0, first[step], second[step])

    def slot(self, me, core, block, orders):
        slot = me & (self.n // 2 - 1)
        for s in range(self.bits - 1):
            away = (block >> (self.bits - 2 - s)) & 1
            slot = slot ^ (away << self.bit_at(core, s, orders))
        return slot


def in_hbm():
    return pl.BlockSpec(memory_space=pltpu.HBM)


def in_vmem():
    return pl.BlockSpec(memory_space=pltpu.VMEM)


def in_smem():
    return pl.BlockSpec(memory_space=pltpu.SMEM)


def held(x):
    return pltpu.with_memory_space_constraint(x, pltpu.VMEM)


def far(x):
    return pltpu.with_memory_space_constraint(x, pltpu.HBM)


def ladder_half(plan, place, multipliers, integrals, keep):
    pairs, depth = multipliers.shape
    slab = integrals.shape[1]
    blocks = slab // LANES // 2
    tile = divisor_at_most(depth, 1024)
    steps = depth // tile
    low = plan.unit.bit_length() - 1
    out_type = F32 if keep else BF16

    def which(i, me, core):
        shift = plan.bit_at(core, 0) - low
        own = (me >> (shift + low)) & 1
        bit = own if keep else 1 - own
        rest = i & ((1 << shift) - 1)
        return ((i >> shift) << (shift + 1)) | (bit << shift) | rest

    def kernel(place_ref, m_ref, i_ref, out_ref, *refs):
        me, core = place_ref[0], place_ref[1]
        if keep:
            m_held, (i_held, total, i_sems) = m_ref, refs
        else:
            m_held, i_held, total, i_sems, m_sems = refs

        def span(k):
            return pl.ds(pl.multiple_of(k * tile, tile), tile)

        def m_copy(k):
            return pltpu.make_async_copy(m_ref.at[:, span(k)], m_held.at[:, span(k)], m_sems.at[k])

        def i_copy(k, i):
            lanes = pl.ds(pl.multiple_of(which(i, me, core) * LANES, LANES), LANES)
            return pltpu.make_async_copy(
                i_ref.at[span(k), lanes],
                i_held.at[span(k), pl.ds(i * LANES, LANES)],
                i_sems.at[k, i],
            )

        for k in range(steps):
            for i in range(blocks):
                i_copy(k, i).start()
            if not keep:
                m_copy(k).start()

        def arrive(k):
            for i in range(blocks):
                i_copy(k, i).wait()
            if not keep:
                m_copy(k).wait()

        def part(k, columns):
            return jnp.dot(m_held[:, span(k)], i_held[span(k), columns], preferred_element_type=F32)

        every = pl.ds(0, blocks * LANES)
        arrive(0)
        total[...] = part(0, every)

        def body(k, carry):
            arrive(k)
            total[...] += part(k, every)
            return carry

        lax.fori_loop(1, steps - 1, body, 0)
        arrive(steps - 1)
        for i in range(blocks):
            lanes = pl.ds(i * LANES, LANES)
            block = (total[:, lanes] + part(steps - 1, lanes)).T
            for t in range(plan.unit):
                away = (which(i, me, core) * plan.unit + t) ^ me
                slot = 0
                for s in range(1, plan.bits):
                    stays = 1 - ((away >> plan.bit_at(core, s)) & 1)
                    slot = slot * 2 + stays
                out_ref[slot] = block[t * plan.rows : (t + 1) * plan.rows].astype(out_type)

    out_shape = [pltpu.VMEM((plan.n // 2, plan.rows, pairs), out_type)]
    scratch = [
        pltpu.VMEM((depth, slab // 2), BF16),
        pltpu.VMEM((pairs, slab // 2), F32),
        pltpu.SemaphoreType.DMA((steps, blocks)),
    ]
    if not keep:
        out_shape.append(pltpu.VMEM((pairs, depth), BF16))
        scratch.append(pltpu.SemaphoreType.DMA((steps,)))
    return pl.pallas_call(
        kernel,
        in_specs=[in_smem(), in_vmem() if keep else in_hbm(), in_hbm()],
        out_specs=[in_vmem()] * len(out_shape),
        out_shape=out_shape,
        scratch_shapes=scratch,
        compiler_params=pltpu.CompilerParams(vmem_limit_bytes=KERNEL_VMEM),
        cost_estimate=pl.CostEstimate(
            flops=pairs * depth * slab,
            bytes_accessed=2 * (pairs * depth + depth * slab // 2 + pairs * slab),
            transcendentals=0,
        ),
        name="ladder_keep" if keep else "ladder_send",
    )(place, (held if keep else far)(multipliers), far(integrals))


def amplitude_part(plan, place, rows, own, other, begin, end, total):
    height, depth = rows.shape
    width = own.shape[1]
    tile = divisor_at_most(width // 4, 1024)
    base, steps = int(width * begin) // tile, int(width * (end - begin)) // tile
    half = depth // 2
    blocks = height // plan.rows

    def kernel(place_ref, l_ref, a_ref, b_ref, *refs):
        o_ref, a_held, b_held, sems = refs[-4:]
        me, core = place_ref[0], place_ref[1]

        def span(j):
            return pl.ds(pl.multiple_of((base + j) * tile, tile), tile)

        def copies(j):
            at = lax.rem(j, 2)
            return (
                pltpu.make_async_copy(a_ref.at[:, span(j)], a_held.at[at], sems.at[0, at]),
                pltpu.make_async_copy(b_ref.at[:, span(j)], b_held.at[at], sems.at[1, at]),
            )

        for c in copies(0):
            c.start()

        def body(j, carry):
            at = lax.rem(j, 2)

            @pl.when(j + 1 < steps)
            def _():
                for c in copies(j + 1):
                    c.start()

            a_copy, b_copy = copies(j)
            a_copy.wait()
            out = jnp.dot(l_ref[:, :half], a_held[at], preferred_element_type=F32)
            b_copy.wait()
            out = out + jnp.dot(l_ref[:, half:], b_held[at], preferred_element_type=F32)
            for i in range(blocks):
                slot = plan.slot(me, core, i, plan.early)
                o_ref[slot, :, span(j)] = out[i * plan.rows : (i + 1) * plan.rows]
            return carry

        lax.fori_loop(0, steps, body, 0)

    given = [] if total is None else [held(total)]
    return pl.pallas_call(
        kernel,
        in_specs=[in_smem(), in_vmem(), in_hbm(), in_hbm()] + [in_vmem()] * len(given),
        out_specs=in_vmem(),
        out_shape=pltpu.VMEM((blocks, plan.rows, width), F32),
        scratch_shapes=[
            pltpu.VMEM((2, half, tile), BF16),
            pltpu.VMEM((2, half, tile), BF16),
            pltpu.SemaphoreType.DMA((2, 2)),
        ],
        input_output_aliases={4: 0} if given else {},
        compiler_params=pltpu.CompilerParams(vmem_limit_bytes=KERNEL_VMEM),
        cost_estimate=pl.CostEstimate(
            flops=2 * height * depth * steps * tile,
            bytes_accessed=(2 * depth + 4 * height) * steps * tile,
            transcendentals=0,
        ),
    )(place, held(rows), far(own), far(other), *given)


def density(plan, place, rows, own, other, total):
    height, depth = sum(r.shape[0] for r in rows), rows[0].shape[1]
    width = own.shape[1]
    tile = divisor_at_most(width, 1024)
    steps = width // tile
    half = depth // 2
    blocks = height // plan.rows
    depth_of_queue = 2

    def kernel(
        place_ref, first_ref, second_ref, a_ref, b_ref, t_ref, o_ref, l_ref, a_held, b_held, o_held, l_sems, in_sems, out_sems
    ):
        me, core = place_ref[0], place_ref[1]

        def span(j):
            return pl.ds(pl.multiple_of(j * tile, tile), tile)

        def copies(j):
            at = lax.rem(j, depth_of_queue)
            return (
                pltpu.make_async_copy(a_ref.at[:, span(j)], a_held.at[at], in_sems.at[0, at]),
                pltpu.make_async_copy(b_ref.at[:, span(j)], b_held.at[at], in_sems.at[1, at]),
            )

        def put(j):
            at = lax.rem(j, 2)
            return pltpu.make_async_copy(o_held.at[at], o_ref.at[:, :, span(j)], out_sems.at[at])

        for c in copies(0):
            c.start()
        cut = first_ref.shape[0]
        joins = (
            pltpu.make_async_copy(first_ref, l_ref.at[pl.ds(0, cut)], l_sems.at[0]),
            pltpu.make_async_copy(second_ref, l_ref.at[pl.ds(cut, height - cut)], l_sems.at[1]),
        )
        for c in joins:
            c.start()
        for c in joins:
            c.wait()

        def body(j, carry):
            at = lax.rem(j, depth_of_queue)

            @pl.when(j + 1 < steps)
            def _():
                for c in copies(j + 1):
                    c.start()

            @pl.when(j >= 2)
            def _():
                put(j - 2).wait()

            a_copy, b_copy = copies(j)
            a_copy.wait()
            out = jnp.dot(l_ref[:, :half], a_held[at], preferred_element_type=F32)
            b_copy.wait()
            out = out + jnp.dot(l_ref[:, half:], b_held[at], preferred_element_type=F32)
            for i in range(blocks):
                slot = plan.slot(me, core, i, plan.orders)
                new = t_ref[slot, :, span(j)] + out[i * plan.rows : (i + 1) * plan.rows]
                o_held[lax.rem(j, 2), slot] = new.astype(BF16)
            put(j).start()
            return carry

        lax.fori_loop(0, steps, body, 0)
        for j in range(max(steps - 2, 0), steps):
            put(j).wait()

    return pl.pallas_call(
        kernel,
        in_specs=[in_smem(), in_vmem(), in_vmem(), in_hbm(), in_hbm(), in_vmem()],
        out_specs=in_hbm(),
        out_shape=jax.ShapeDtypeStruct((blocks, plan.rows, width), BF16),
        scratch_shapes=[
            pltpu.VMEM((height, depth), BF16),
            pltpu.VMEM((depth_of_queue, half, tile), BF16),
            pltpu.VMEM((depth_of_queue, half, tile), BF16),
            pltpu.VMEM((2, blocks, plan.rows, tile), BF16),
            pltpu.SemaphoreType.DMA((2,)),
            pltpu.SemaphoreType.DMA((2, depth_of_queue)),
            pltpu.SemaphoreType.DMA((2,)),
        ],
        compiler_params=pltpu.CompilerParams(vmem_limit_bytes=KERNEL_VMEM),
        cost_estimate=pl.CostEstimate(
            flops=2 * height * depth * width,
            bytes_accessed=2 * depth * width + 2 * height * width,
            transcendentals=0,
        ),
        name="density",
    )(place, *map(held, rows), far(own), far(other), held(total)).reshape(height, width)


def renew_slab(current, ladder, rest, virtual, occupied):
    divisor = virtual.astype(F32)[:, None] - occupied.astype(F32)[None, :]
    renewed = current.astype(F32) + (ladder + rest.astype(F32)) / divisor
    return renewed.astype(BF16)


def split(total):
    half = total.shape[0] // 2
    return total[:half].astype(BF16), total[half:]


def both_cores(plan, here, mine, across):
    stays = jnp.where(here > 0, mine, across)
    leaves = jnp.where(here > 0, across, mine)
    return jnp.concatenate([stays, plan.swap(leaves)], axis=1)


def local(
    plan,
    multipliers,
    integrals,
    amplitudes,
    slab_multipliers,
    slab_amplitudes,
    residual_rest,
    occupied_energy,
    virtual_energy,
):
    after = lax.optimization_barrier
    last = plan.bits - 1
    me, core = lax.axis_index("vp"), lax.axis_index("op")
    here = jnp.full(slab_amplitudes.shape, core == me // (plan.n // 2), F32)
    place, here = after((jnp.stack([me, core]).astype(jnp.int32), here))
    across = plan.exchange(slab_amplitudes, last)
    sent, in_reach = ladder_half(plan, place, multipliers, integrals, keep=False)
    later, across, sent = after((place, across, sent))
    arrived = plan.exchange(sent, 0)
    amp = both_cores(plan, here, slab_amplitudes, across)
    amp, to_swap = after((amp, in_reach))
    their_multipliers = plan.swap(to_swap)
    amp_next = plan.exchange(amp, last - 1, plan.early)
    (kept,) = ladder_half(plan, later, in_reach, integrals, keep=True)
    kept, amp_next, to_swap = after((kept, amp_next, amplitudes))
    their_amplitudes = plan.swap(to_swap)
    amp = jnp.concatenate([amp, amp_next], axis=0)
    waiting = list(range(last - 2, -1, -1))
    for step in range(1, plan.bits):
        sent, kept = split(kept + arrived.astype(F32))
        if step > 1 and len(waiting) > 1:
            amp_next = plan.exchange(amp, waiting.pop(0), plan.early)
            amp = jnp.concatenate([amp, amp_next], axis=0)
            sent, amp = after((sent, amp))
        arrived = plan.exchange(sent, step)
    for step in waiting:
        amp = jnp.concatenate([amp, plan.exchange(amp, step, plan.early)], axis=0)
    ladder = (kept + arrived.astype(F32)).reshape(kept.shape[-2:])
    renewed = renew_slab(slab_multipliers, ladder, residual_rest, virtual_energy, occupied_energy)

    part = functools.partial(amplitude_part, plan, place, amp, multipliers, their_multipliers)
    across = plan.exchange(renewed, last)
    across, total = after((across, part(0, 0.25, None)))
    rows = both_cores(plan, here, renewed, across)
    for step in range(last - 1, -1, -1):
        rows_next = plan.exchange(rows, step)
        if step == 1:
            rows_next, total, their_amplitudes = after((rows_next, part(0.25, 0.5, total), their_amplitudes))
        if step == 0:
            rows_next, total = after((rows_next, part(0.5, 1.0, total)))
            break
        rows = jnp.concatenate([rows, rows_next], axis=0)
    return renewed, density(plan, place, (rows, rows_next), amplitudes, their_amplitudes, total)


def solution(mesh):
    def whole(*args):
        plan = Plan(mesh, args[1].shape[1])

        def body(*blocks):
            return local(plan, *blocks)

        return jax.shard_map(
            body,
            mesh=mesh,
            in_specs=(
                P("op", "vp"),
                P("vp", None),
                P("op", "vp"),
                P("vp", "op"),
                P("vp", "op"),
                P("vp", "op"),
                P("op"),
                P("vp"),
            ),
            out_specs=(P("vp", "op"), P("op", "vp")),
            check_vma=False,
        )(*args)

    return whole
```
